512 devices in a mesh: row: 16 (over z), col: 8 (over x, core), layer: 4 (over y).
Axes of the slice: x: 4, y: 4, z: 16, core: 2. Of those that a mesh axis runs over, the one named last changes fastest.
Arguments:
- p_slabs: bfloat16 [4, 4096, 1024], P('layer', 'row', 'col'), may hold values from -0.09375 to 0.09375
- p_mask: int32 [4, 128, 32], P('layer', 'row', 'col'), may hold values 0 or 1
- h_slabs: bfloat16 [4, 1024, 4096], P('layer', 'row', 'col'), may hold values from -12 to 12
- h_mask: int32 [4, 32, 128], P('layer', 'row', 'col'), may hold values from 0 to 1, as said below
- gauss_row: int32 [524288], P(('row', 'col', 'layer')), may hold values from 0 to 255
- gauss_col: int32 [524288], P(('row', 'col', 'layer')), may hold values from 0 to 4095
- gauss_cell: int32 [524288], P(('row', 'col', 'layer')), may hold values from 0 to 32767
- gauss_expo: float32 [524288], P(('row', 'col', 'layer')), may hold values from 0.05 to 0.6
- gauss_pref: float32 [524288], P(('row', 'col', 'layer')), may hold values from -384 to 384
Outputs:
- product: bfloat16 [4096, 4096], P('row', ('col', 'layer'))
- density: float32 [256, 128, 512], P('row', 'col', 'layer')
The draws below stay inside these ranges and needn't reach their ends.
Inputs may be any that keep to these rules, and one draw needn't show every extreme that they name: Each device's tile of h_mask (block rows l, r * 2 to r * 2 + 1, block columns c * 16 to c * 16 + 15) has at most 16 ones; some tile has exactly 16.
All inputs are finite; a program needn't handle non-finite values. No bound on the sum of `p_mask` on one device may be relied on, other than what follows from the above.
Results may differ from the reference program's by a relative error of at most 0.001.
Values may be sent and summed in bfloat16 or wider, within the bound.
A program may use at most 64 MiB of HBM per device.

```python
import math
import jax
import jax.numpy as jnp
from jax import lax

BS = 32
HB = 2
N = 4096
LAYERS = 4
HCB = 16
HCAP = 16
BAND = 256
GX = 16
GY = 16
GZ = 128
R = 4
NG = 1024
GAUSS = 524288
N_ROW = 16
N_COL = 8
N_LAYER = 4


def draw_h_mask(key, part):
    row_tiles = N // (LAYERS * BS * HB)
    col_tiles = N // BS // HCB
    tiles = LAYERS * row_tiles * col_tiles
    blocks = HB * HCB
    count_key = jax.random.fold_in(key, 11)
    pick_key = jax.random.fold_in(key, 12)
    perm_key = jax.random.fold_in(key, 13)
    counts = jax.random.randint(count_key, (tiles,), HCAP // 2, HCAP + 1)
    full_tile = jax.random.randint(pick_key, (), 0, tiles)
    counts = counts.at[full_tile].set(HCAP)
    keys = jax.random.split(perm_key, tiles)

    def one_tile(tile_key, count):
        order = jax.random.permutation(tile_key, blocks)
        rank = jnp.zeros((blocks,), jnp.int32).at[order].set(jnp.arange(blocks, dtype=jnp.int32))
        return (rank < count).astype(jnp.int32)
    flat = jax.vmap(one_tile)(keys, counts)
    grid = flat.reshape(LAYERS, row_tiles, col_tiles, HB, HCB)
    return jnp.transpose(grid, (0, 1, 3, 2, 4)).reshape(LAYERS, row_tiles * HB, col_tiles * HCB)


def with_ends(entries, stream_key, low, high):
    spot = [jax.random.randint(jax.random.fold_in(stream_key, axis), (), 0, length) for axis, length in enumerate(entries.shape)]
    main_axis = entries.shape.index(max(entries.shape))
    beside = spot[:main_axis] + [(spot[main_axis] + 1) % entries.shape[main_axis]] + spot[main_axis + 1:]
    return entries.at[tuple(spot)].set(low).at[tuple(beside)].set(high)


def block_scale(own_key, shape, pieces, low, largest):
    loudness = 1.0
    for axis_at, blocks in pieces:
        heights = jax.random.uniform(jax.random.fold_in(jax.random.fold_in(own_key, 6), axis_at), (blocks,), jnp.float32, low / len(pieces), largest / len(pieces))
        loudness = loudness * jnp.repeat(jnp.exp(heights), shape[axis_at] // blocks).reshape((-1,) + (1,) * (len(shape) - 1 - axis_at))
    return loudness


def bell_draw(key, extent, scale, limit, pieces=(), kind=jnp.bfloat16):
    values = scale * jax.random.normal(key, extent, jnp.float32)
    if pieces:
        values = values * block_scale(key, extent, pieces, -0.22, 0.18)
    return jnp.clip(values, -limit, limit).astype(kind)


def setup_inputs(seed: int = 0) -> dict:
    arg_keys = jax.random.split(jax.random.key(seed), 10)
    p_slabs = bell_draw(arg_keys[0], (LAYERS, N, N // LAYERS), N ** -0.5, 0.09375, ((0, 4), (1, 16), (2, 8)))
    p_mask = with_ends((jax.random.randint(arg_keys[1], (LAYERS, N // BS, N // (LAYERS * BS)), 0, 2) < 1).astype(jnp.int32), jax.random.fold_in(arg_keys[1], 1), 0, 1)
    h_slabs = bell_draw(arg_keys[2], (LAYERS, N // LAYERS, N), 2.0, 12.0, ((0, 4), (1, 16), (2, 8)))
    h_mask = draw_h_mask(jax.random.fold_in(arg_keys[9], 71), 0)
    gauss_row = with_ends(jax.random.randint(arg_keys[4], (GAUSS,), 0, BAND), jax.random.fold_in(arg_keys[4], 1), 0, BAND - 1).astype(jnp.int32)
    gauss_col = with_ends(jax.random.randint(arg_keys[5], (GAUSS,), 0, N), jax.random.fold_in(arg_keys[5], 1), 0, N - 1).astype(jnp.int32)
    gauss_cell = with_ends(jax.random.randint(arg_keys[6], (GAUSS,), 0, GX * GY * GZ), jax.random.fold_in(arg_keys[6], 1), 0, (GX * GY * GZ) - 1).astype(jnp.int32)
    gauss_expo = jnp.clip(jnp.exp(math.log(0.6) - 2.4849067 * jax.random.uniform(arg_keys[7], (GAUSS,), jnp.float32) ** block_scale(arg_keys[7], (GAUSS,), ((0, 512),), -0.2, 0.2)), 0.05, 0.6)
    gauss_pref = bell_draw(arg_keys[8], (GAUSS,), (N // 64), 384.0, ((0, 512),), jnp.float32)
    return dict(p_slabs=p_slabs, p_mask=p_mask, h_slabs=h_slabs, h_mask=h_mask, gauss_row=gauss_row, gauss_col=gauss_col, gauss_cell=gauss_cell, gauss_expo=gauss_expo, gauss_pref=gauss_pref)


def expand(mask):
    return jnp.repeat(jnp.repeat(mask, BS, axis=1), BS, axis=2) > 0


def profile(center, expo, length):
    pos = jnp.arange(length + 2 * R, dtype=jnp.int32) - R
    dist = pos[:, None] - center[None, :]
    dist_f = dist.astype(jnp.float32)
    value = jnp.exp(-expo[None, :] * dist_f * dist_f)
    return jnp.where(jnp.abs(dist) <= R, value, jnp.zeros_like(value))


def collocate(cell, expo, coef):
    cx = cell // (GY * GZ)
    cy = (cell // GZ) % GY
    cz = cell % GZ
    ex = profile(cx, expo, GX)
    ey = profile(cy, expo, GY)
    ez = profile(cz, expo, GZ)
    plane = (ex[:, None, :] * ey[None, :, :]).reshape((GX + 2 * R) * (GY + 2 * R), -1)
    depth = ez * coef[None, :]
    dens = lax.dot_general(plane, depth, (((1,), (1,)), ((), ())), precision=lax.Precision.HIGHEST, preferred_element_type=jnp.float32)
    return dens.reshape(GX + 2 * R, GY + 2 * R, GZ + 2 * R)


def fold(bricks, dev_axis, cell_axis, cells):
    core = lax.slice_in_dim(bricks, R, R + cells, axis=cell_axis)
    low = lax.slice_in_dim(jnp.roll(bricks, 1, dev_axis), cells + R, cells + 2 * R, axis=cell_axis)
    high = lax.slice_in_dim(jnp.roll(bricks, -1, dev_axis), 0, R, axis=cell_axis)
    widths_low = [(0, 0)] * bricks.ndim
    widths_low[cell_axis] = (0, cells - R)
    widths_high = [(0, 0)] * bricks.ndim
    widths_high[cell_axis] = (cells - R, 0)
    return core + jnp.pad(low, widths_low) + jnp.pad(high, widths_high)


def reference(p_slabs, p_mask, h_slabs, h_mask, gauss_row, gauss_col, gauss_cell, gauss_expo, gauss_pref):
    p_eff = jnp.where(expand(p_mask), p_slabs, jnp.zeros_like(p_slabs)).astype(jnp.float32)
    p_mat = jnp.transpose(p_eff, (1, 0, 2)).reshape(N, N)
    h_mat = jnp.where(expand(h_mask), h_slabs, jnp.zeros_like(h_slabs)).astype(jnp.float32).reshape(N, N)
    product = jnp.dot(p_mat, h_mat, precision=lax.Precision.HIGHEST, preferred_element_type=jnp.float32).astype(jnp.bfloat16)
    devices = N_ROW * N_COL * N_LAYER
    band_rows = N // N_ROW
    rows_in = gauss_row.reshape(devices, NG)
    cols_in = gauss_col.reshape(devices, NG)
    cell = gauss_cell.reshape(devices, NG)
    expo = gauss_expo.reshape(devices, NG)
    pref = gauss_pref.reshape(devices, NG)

    def brick(index):
        r_pos = index // (N_COL * N_LAYER)
        grow = r_pos * band_rows + rows_in[index]
        gcol = cols_in[index]
        coef = pref[index] * p_mat[grow, gcol]
        return collocate(cell[index], expo[index], coef)

    bricks = lax.map(brick, jnp.arange(devices, dtype=jnp.int32))
    bricks = bricks.reshape(N_ROW, N_COL, N_LAYER, GX + 2 * R, GY + 2 * R, GZ + 2 * R)
    bricks = fold(bricks, 0, 3, GX)
    bricks = fold(bricks, 1, 4, GY)
    bricks = fold(bricks, 2, 5, GZ)
    density = jnp.transpose(bricks, (0, 3, 1, 4, 2, 5)).reshape(GX * N_ROW, GY * N_COL, GZ * N_LAYER)
    return product, density
```

```python
import jax
import jax.numpy as jnp
from jax import lax
from jax.experimental import pallas as pl
from jax.experimental.pallas import tpu as pltpu
from jax.sharding import PartitionSpec as P

BS = 32
GX = 16
GY = 16
GZ = 128
R = 4
NG = 1024
NR = 16
NC = 8
NL = 4
EX = GX + 2 * R
EY = GY + 2 * R
F32 = jnp.float32
BF16 = jnp.bfloat16


def kernel(
    p_ref, h_ref, g_ref, prod_ref, dens_ref,
    pall, hall, gpad, gcols, onehot, colb, acc, ez, plane_hi, plane_lo, dens, rim, rim_in, row_in, col_in,
    send, recv, local,
):
    r = lax.axis_index("row")
    c = lax.axis_index("col")
    l = lax.axis_index("layer")
    row_of = lambda d: lax.rem(r + (d + NR), NR)
    col_of = lambda d: lax.rem(c + (d + NC), NC)
    lay_of = lambda d: lax.rem(l + (d + NL), NL)
    odd = lax.rem(c, 2)
    sib = c + 1 - 2 * odd
    out = c - 1 + 2 * odd
    other = lax.rem(out + NC, NC)

    barrier = pltpu.get_barrier_semaphore()
    peers = (
        [{"layer": lay_of(d)} for d in (1, 2, 3)]
        + [{"col": col_of(2 * d)} for d in (1, 2, 3)]
        + [{"col": sib}, {"col": other}, {"row": row_of(1)}, {"row": row_of(-1)}]
    )
    for peer in peers:
        pl.semaphore_signal(barrier, inc=1, device_id=peer, device_id_type=pl.DeviceIdType.MESH)
    pl.semaphore_wait(barrier, len(peers))

    pending = []
    slots = {}

    def push(key, src, dst, peer):
        n = slots.setdefault(key, len(slots))
        copy = pltpu.make_async_remote_copy(
            src_ref=src, dst_ref=dst, send_sem=send.at[n], recv_sem=recv.at[n],
            device_id=peer, device_id_type=pl.DeviceIdType.MESH,
        )
        copy.start()
        pending.append(copy)
        return copy

    low = pl.ds(0, 128)
    high = pl.ds(128, 128)
    copies = {}
    own_p = pltpu.make_async_copy(p_ref, pall.at[c, l], local.at[0])
    own_p.start()
    own_h = pltpu.make_async_copy(h_ref.at[l], hall.at[l, r], local.at[1])
    own_h.start()
    for d in (1, 3, 2):
        copies["ha", d] = push(("ha", d), h_ref.at[lay_of(d)], hall.at[l, r], {"layer": lay_of(d)})
    for d in (1, 3, 2):
        copies["py", d] = push(("py", d), p_ref, pall.at[c, l], {"layer": lay_of(d)})
        copies["px", d] = push(("px", d), p_ref, pall.at[c, l], {"col": col_of(2 * d)})
    copies["ps"] = push(("ps",), p_ref, pall.at[c, l], {"col": sib})

    gpad[0:8, :] = g_ref[...]
    gpad[8:128, :] = jnp.zeros((120, NG), F32)
    for k in range(NG // 128):
        gcols[k * 128 : (k + 1) * 128, :] = jnp.transpose(gpad[0:128, k * 128 : (k + 1) * 128])

    def prepare(k, _):
        rows = pl.ds(pl.multiple_of(k * 128, 128), 128)
        g = gcols[rows, :]
        lane = lax.broadcasted_iota(jnp.int32, (128, 256), 1)
        onehot[rows, :] = jnp.where(g[:, 0:1] == lane.astype(F32), 1.0, 0.0).astype(BF16)
        colb[rows, :] = g[:, 1:2] - lane[:, :128].astype(F32)
        pos = jnp.where(lane < 136, lane, lane - 144).astype(F32)
        dist = pos - g[:, 2:3]
        keep = (jnp.abs(dist) <= R) & ((lane < 132) | ((lane >= 140) & (lane < 144)))
        ez[rows, :] = jnp.where(keep, jnp.exp(-g[:, 3:4] * dist * dist), 0.0)
        acc[rows, :] = jnp.zeros((128, 128), F32)
        return 0

    lax.fori_loop(0, NG // 128, prepare, 0)

    own_h.wait()
    for d in (1, 3, 2):
        copies["ha", d].wait_recv()
    right = {"row": row_of(1)}
    left = {"row": row_of(-1)}
    copies["hr", 0] = push(("hr", 0), hall.at[:, r], hall.at[:, r], right)
    copies["hl", 0] = push(("hl", 0), hall.at[:, r], hall.at[:, r], left)

    def ring(s):
        copies["hr", s - 1].wait_recv()
        if s < NR // 2:
            piece = hall.at[:, row_of(-s)]
            copies["hr", s] = push(("hr", s), piece, piece, right)
        if s < NR // 2:
            copies["hl", s - 1].wait_recv()
        if s < NR // 2 - 1:
            piece = hall.at[:, row_of(s)]
            copies["hl", s] = push(("hl", s), piece, piece, left)

    def lookup(tiles):
        refs = [(pall.at[a, b], (b * NG + a * 128).astype(F32)) for a, b in tiles]

        def body(k, _):
            rows = pl.ds(pl.multiple_of(k * 256, 256), 256)
            hot = onehot[rows, :]
            want = colb[rows, :]
            total = acc[rows, :]
            for ref, base in refs:
                found = jnp.dot(hot, ref[...], preferred_element_type=F32)
                total = total + jnp.where(want == base, found, 0.0)
            acc[rows, :] = total
            return 0

        lax.fori_loop(0, NG // 256, body, 0)

    for d in (1, 3, 2):
        copies["py", d].wait_recv()
        tile = pall.at[c, lay_of(-d)]
        for e in (1, 3, 2):
            part = tile.at[low]
            copies["a", d, e] = push(("a", d, e), part, part, {"col": col_of(2 * e)})
        copies["sy", d] = push(("sy", d), tile, tile, {"col": sib})
        copies["px", d].wait_recv()
        tile = pall.at[col_of(-2 * d), l]
        for e in (1, 3, 2):
            part = tile.at[high]
            copies["b", d, e] = push(("b", d, e), part, part, {"layer": lay_of(e)})
        copies["sx", d] = push(("sx", d), tile, tile, {"col": sib})
    own_p.wait()

    ring(1)
    pos = lax.broadcasted_iota(jnp.int32, (EX, NG), 0)
    pos = jnp.where(pos < 20, pos, pos - 24).astype(F32)
    expo = g_ref[3:4, :]
    dx = pos - g_ref[5:6, :]
    ex = jnp.where(jnp.abs(dx) <= R, jnp.exp(-expo * dx * dx), 0.0)
    dy = pos - g_ref[6:7, :]
    ey = jnp.where(jnp.abs(dy) <= R, jnp.exp(-expo * dy * dy), 0.0)
    for i in range(EX):
        value = ex[i : i + 1, :] * ey
        upper = value.astype(BF16)
        plane_hi[i * EY : (i + 1) * EY, :] = upper
        plane_lo[i * EY : (i + 1) * EY, :] = (value - upper.astype(F32)).astype(BF16)
    lookup([(c, l)] + [(c, lay_of(-d)) for d in (1, 3, 2)] + [(col_of(-2 * d), l) for d in (1, 3, 2)])
    ring(2)

    copies["ps"].wait_recv()
    for d in (1, 3, 2):
        copies["sy", d].wait_recv()
        copies["sx", d].wait_recv()
    sib_of = lambda d: lax.rem(sib + (d + NC), NC)
    lookup([(sib, l)] + [(sib, lay_of(-d)) for d in (1, 3, 2)] + [(sib_of(-2 * d), l) for d in (1, 3, 2)])
    ring(3)

    for d in (1, 3, 2):
        for e in (1, 3, 2):
            copies["a", d, e].wait_recv()
            part = pall.at[col_of(-2 * e), lay_of(-d), low]
            copies["sa", d, e] = push(("sa", d, e), part, part, {"col": sib})
            copies["b", d, e].wait_recv()
            part = pall.at[col_of(-2 * d), lay_of(-e), high]
            copies["sb", d, e] = push(("sb", d, e), part, part, {"col": sib})
    corners = [(d, e) for d in (1, 3, 2) for e in (1, 3, 2)]
    lookup([(col_of(-2 * d), lay_of(-e)) for d, e in corners])
    ring(4)
    for d, e in corners:
        copies["sa", d, e].wait_recv()
        copies["sb", d, e].wait_recv()
    lookup([(sib_of(-2 * d), lay_of(-e)) for d, e in corners])
    ring(5)

    def deepen(k, _):
        rows = pl.ds(pl.multiple_of(k * 128, 128), 128)
        coef = jnp.sum(acc[rows, :], axis=1, keepdims=True) * gcols[rows, 4:5]
        ez[rows, :] = ez[rows, :] * coef
        return 0

    lax.fori_loop(0, NG // 128, deepen, 0)
    depth = ez[...]
    depth_hi = depth.astype(BF16)
    depth_lo = (depth - depth_hi.astype(F32)).astype(BF16)
    step = 4 * EY
    for k in range(EX // 4):
        rows = slice(k * step, (k + 1) * step)
        part = jnp.dot(plane_hi[rows, :], depth_lo, preferred_element_type=F32)
        part = part + jnp.dot(plane_lo[rows, :], depth_hi, preferred_element_type=F32)
        part = part + jnp.dot(plane_hi[rows, :], depth_hi, preferred_element_type=F32)
        dens[k * 4 : (k + 1) * 4] = part[:, :128].reshape(4, EY, 128)
        gpad[rows, 0:128] = part[:, 128:]
    gpad[EX * EY : 640, 0:128] = jnp.zeros((64, 128), F32)
    for k in range(5):
        turned = jnp.transpose(gpad[k * 128 : (k + 1) * 128, 0:128])
        rim[:, k * 128 : (k + 1) * 128] = turned[0:16, :]
    rim_in[8:120, :] = jnp.zeros((112, 640), F32)
    up = {"layer": lay_of(1)}
    down = {"layer": lay_of(-1)}
    copies["lu"] = push(("lu",), rim.at[0:8], rim_in.at[0:8], up)
    copies["ld"] = push(("ld",), rim.at[8:16], rim_in.at[120:128], down)
    ring(6)

    copies["lu"].wait_recv()
    copies["ld"].wait_recv()
    for k in range(5):
        gpad[k * 128 : (k + 1) * 128, 0:128] = jnp.transpose(rim_in[:, k * 128 : (k + 1) * 128])
    for k in range(EX):
        dens[k] = dens[k] + gpad[k * EY : (k + 1) * EY, 0:128]
    copies["ru"] = push(("ru",), dens.at[16:20], row_in.at[0], right)
    copies["rd"] = push(("rd",), dens.at[20:24], row_in.at[1], left)
    ring(7)

    copies["ru"].wait_recv()
    copies["rd"].wait_recv()
    dens[0:4] = dens[0:4] + row_in[0]
    dens[12:16] = dens[12:16] + row_in[1]
    edge = dens.at[0:16, 16:24]
    copies["cu"] = push(("cu",), edge, col_in.at[0], {"col": col_of(1)})
    copies["cd"] = push(("cd",), edge, col_in.at[1], {"col": col_of(-1)})
    ring(8)

    total = jnp.zeros((256, 128), F32)
    for b in range(NL):
        for k in range(NC // 2):
            lhs = jnp.concatenate([pall[2 * k, b], pall[2 * k + 1, b]], axis=1)
            rhs = hall[b, 4 * k : 4 * k + 4].reshape(256, 128)
            total = total + jnp.dot(lhs, rhs, preferred_element_type=F32)
    prod_ref[...] = total.astype(BF16)

    copies["cu"].wait_recv()
    copies["cd"].wait_recv()
    inner = lax.broadcasted_iota(jnp.int32, (16, 8, 128), 1)
    dens_ref[:, 0:8, :] = dens[0:16, 0:8, :] + jnp.where(inner < 4, col_in[0], 0.0)
    dens_ref[:, 8:16, :] = dens[0:16, 8:16, :] + jnp.where(inner >= 4, col_in[1], 0.0)
    for copy in pending:
        copy.wait_send()


def expand_mask(mask, block):
    return jnp.repeat(jnp.repeat(mask, block, axis=0), block, axis=1) > 0


def on_device(
    p_slabs, p_mask, h_slabs, h_mask, gauss_row, gauss_col, gauss_cell, gauss_expo, gauss_pref
):
    p_local = jnp.where(expand_mask(p_mask[0], BS), p_slabs[0], jnp.zeros_like(p_slabs[0]))
    h_local = jnp.where(expand_mask(h_mask[0], BS), h_slabs[0], jnp.zeros_like(h_slabs[0]))
    h_parts = jnp.transpose(h_local.reshape(64, NL, 128), (1, 0, 2))
    cx = gauss_cell // (GY * GZ)
    cy = gauss_cell // GZ % GY
    cz = gauss_cell % GZ
    gauss = jnp.stack(
        [gauss_row.astype(F32), gauss_col.astype(F32), cz.astype(F32), gauss_expo, gauss_pref,
         cx.astype(F32), cy.astype(F32), jnp.zeros_like(gauss_expo)]
    )
    n_sem = 80
    vmem = pl.BlockSpec(memory_space=pltpu.VMEM)
    return pl.pallas_call(
        kernel,
        out_shape=(
            jax.ShapeDtypeStruct((256, 128), BF16),
            jax.ShapeDtypeStruct((GX, GY, GZ), F32),
        ),
        in_specs=[vmem] * 3,
        out_specs=(vmem, vmem),
        scratch_shapes=[
            pltpu.VMEM((NC, NL, 256, 128), BF16),
            pltpu.VMEM((NL, NR, 64, 128), BF16),
            pltpu.VMEM((640, NG), F32),
            pltpu.VMEM((NG, 128), F32),
            pltpu.VMEM((NG, 256), BF16),
            pltpu.VMEM((NG, 128), F32),
            pltpu.VMEM((NG, 128), F32),
            pltpu.VMEM((NG, 256), F32),
            pltpu.VMEM((EX * EY, NG), BF16),
            pltpu.VMEM((EX * EY, NG), BF16),
            pltpu.VMEM((EX, EY, 128), F32),
            pltpu.VMEM((16, 640), F32),
            pltpu.VMEM((128, 640), F32),
            pltpu.VMEM((2, 4, EY, 128), F32),
            pltpu.VMEM((2, 16, 8, 128), F32),
            pltpu.SemaphoreType.DMA((n_sem,)),
            pltpu.SemaphoreType.DMA((n_sem,)),
            pltpu.SemaphoreType.DMA((2,)),
        ],
        compiler_params=pltpu.CompilerParams(collective_id=0, has_side_effects=True),
    )(p_local, h_parts, gauss)


def solution(mesh):
    placed = (
        P("layer", "row", "col"),
        P("layer", "row", "col"),
        P("layer", "row", "col"),
        P("layer", "row", "col"),
        P(("row", "col", "layer")),
        P(("row", "col", "layer")),
        P(("row", "col", "layer")),
        P(("row", "col", "layer")),
        P(("row", "col", "layer")),
    )
    return jax.shard_map(
        on_device,
        mesh=mesh,
        in_specs=placed,
        out_specs=(P("row", ("col", "layer")), P("row", "col", "layer")),
        check_vma=False,
    )
```

```python
import jax
import jax.numpy as jnp
from jax import lax
from jax.experimental import pallas as pl
from jax.experimental.pallas import tpu as pltpu
from jax.sharding import PartitionSpec as P

BS = 32
GX = 16
GY = 16
GZ = 128
R = 4
NG = 1024
NR = 16
NC = 8
NL = 4
EX = GX + 2 * R
EY = GY + 2 * R
F32 = jnp.float32
BF16 = jnp.bfloat16


def kernel(
    p_hbm, pm_hbm, h_hbm, hm_hbm, row_hbm, gcol_hbm, cell_hbm, expo_hbm, pref_hbm, prod_ref, dens_ref,
    p_in, pm_in, h_in, hm_in, g_int, g_float, h_ref, turn, pall, hall, gpad, gcols, onehot, colb, acc, ez, plane_hi, plane_lo, dens, rim, rim_in, row_in, col_in,
    send, recv, local,
):
    r = lax.axis_index("row")
    c = lax.axis_index("col")
    l = lax.axis_index("layer")
    row_of = lambda d: lax.rem(r + (d + NR), NR)
    col_of = lambda d: lax.rem(c + (d + NC), NC)
    lay_of = lambda d: lax.rem(l + (d + NL), NL)
    odd = lax.rem(c, 2)
    sib = c + 1 - 2 * odd
    out = c - 1 + 2 * odd
    other = lax.rem(out + NC, NC)

    loads = [
        pltpu.make_async_copy(src, dst, local.at[2 + n])
        for n, (src, dst) in enumerate(
            [(p_hbm, p_in), (pm_hbm, pm_in), (h_hbm, h_in), (hm_hbm, hm_in), (row_hbm, g_int.at[0]), (gcol_hbm, g_int.at[1]),
             (cell_hbm, g_int.at[2]), (expo_hbm, g_float.at[0]), (pref_hbm, g_float.at[1])]
        )
    ]
    for copy in loads:
        copy.start()
    barrier = pltpu.get_barrier_semaphore()
    peers = (
        [{"layer": lay_of(d)} for d in (1, 2, 3)]
        + [{"col": col_of(2 * d)} for d in (1, 2, 3)]
        + [{"col": sib}, {"col": other}, {"row": row_of(1)}, {"row": row_of(-1)}]
    )
    for peer in peers:
        pl.semaphore_signal(barrier, inc=1, device_id=peer, device_id_type=pl.DeviceIdType.MESH)
    block = lax.broadcasted_iota(jnp.int32, (4, 128), 0)
    of_lane = lax.broadcasted_iota(jnp.int32, (4, 128), 1) // BS
    loads[0].wait()
    loads[1].wait()
    for i in range(256 // BS):
        column = jnp.broadcast_to(pm_in[:, i : i + 1], (4, 128))
        keep = jnp.sum(jnp.where(block == of_lane, column, 0), axis=0, keepdims=True) > 0
        rows = slice(i * BS, (i + 1) * BS)
        value = jnp.where(jnp.broadcast_to(keep, (BS, 128)), p_in[rows, :].astype(F32), 0.0)
        pall[c, l, rows, :] = value.astype(BF16)
    loads[2].wait()
    loads[3].wait()
    of_lane = lax.broadcasted_iota(jnp.int32, (1, 128), 1) // BS
    for q in range(NL):
        for i in range(64 // BS):
            keep = jnp.zeros((1, 128), jnp.int32)
            for j in range(4):
                at = q * 4 + j
                keep = jnp.where(of_lane == j, jnp.broadcast_to(hm_in[i : i + 1, at : at + 1], (1, 128)), keep)
            rows = slice(i * BS, (i + 1) * BS)
            value = h_in[rows, q * 128 : (q + 1) * 128].astype(F32)
            value = jnp.where(jnp.broadcast_to(keep > 0, (BS, 128)), value, 0.0)
            h_ref[q, rows, :] = value.astype(BF16)
    own_h = pltpu.make_async_copy(h_ref.at[l], hall.at[l, r], local.at[1])
    own_h.start()
    p_ref = pall.at[c, l]
    pl.semaphore_wait(barrier, len(peers))

    pending = []
    slots = {}

    def push(key, src, dst, peer):
        n = slots.setdefault(key, len(slots))
        copy = pltpu.make_async_remote_copy(
            src_ref=src, dst_ref=dst, send_sem=send.at[n], recv_sem=recv.at[n],
            device_id=peer, device_id_type=pl.DeviceIdType.MESH,
        )
        copy.start()
        pending.append(copy)
        return copy

    low = pl.ds(0, 128)
    high = pl.ds(128, 128)
    copies = {}
    right = {"row": row_of(1)}
    left = {"row": row_of(-1)}
    order = (0, 1, 3, 2)
    last = NR // 2 - 1
    for d in (1, 3, 2):
        copies["ha", d] = push(("ha", d), h_ref.at[lay_of(d)], hall.at[l, r], {"layer": lay_of(d)})
    own_h.wait()
    piece = hall.at[l, r]
    copies["hr", 0, 0] = push(("hr", 0, 0), piece, piece, right)
    copies["hl", 0, 0] = push(("hl", 0, 0), piece, piece, left)
    for d in (1, 3, 2):
        copies["py", d] = push(("py", d), p_ref, pall.at[c, l], {"layer": lay_of(d)})
        copies["px", d] = push(("px", d), p_ref, pall.at[c, l], {"col": col_of(2 * d)})
    copies["ps"] = push(("ps",), p_ref, pall.at[c, l], {"col": sib})

    for copy in loads[4:]:
        copy.wait()
    cell = g_int[2]
    turn[0:8, :] = g_int[0].astype(F32)
    turn[8:16, :] = g_int[1].astype(F32)
    turn[16:24, :] = (cell & (GZ - 1)).astype(F32)
    turn[24:32, :] = g_float[0]
    turn[32:40, :] = g_float[1]
    turn[40:128, :] = jnp.zeros((88, 128), F32)
    gcols[...] = jnp.transpose(turn[...])

    def ring_start():
        for d in order[1:]:
            copies["ha", d].wait_recv()
            piece = hall.at[lay_of(-d), r]
            copies["hr", 0, d] = push(("hr", 0, d), piece, piece, right)
            copies["hl", 0, d] = push(("hl", 0, d), piece, piece, left)

    def ring(s):
        for d in order:
            for way, sign, peer, extra in (("hr", -1, right, (0, 1)), ("hl", 1, left, (3, 2))):
                if (way, s - 1, d) in copies:
                    copies[way, s - 1, d].wait_recv()
                    if s < last or (s == last and d in extra):
                        piece = hall.at[lay_of(-d), row_of(sign * s)]
                        copies[way, s, d] = push((way, s, d), piece, piece, peer)

    ring_start()
    lane = lax.broadcasted_iota(jnp.int32, (128, 256), 1)
    lane_f = lane.astype(F32)
    pos_z = jnp.where(lane < 136, lane, lane - 144).astype(F32)
    near_z = (lane < 132) | ((lane >= 140) & (lane < 144))
    for k in range(NG // 128):
        rows = slice(k * 128, (k + 1) * 128)
        onehot[rows, :] = jnp.where(gcols[:, k : k + 1] == lane_f, 1.0, 0.0).astype(BF16)
        colb[rows, :] = gcols[:, 8 + k : 9 + k] - lane_f[:, :128]
        acc[rows, :] = jnp.zeros((128, 128), F32)

    def lookup(tiles):
        refs = [(pall.at[a, b], (b * NG + a * 128).astype(F32)) for a, b in tiles]

        def body(k, _):
            rows = pl.ds(pl.multiple_of(k * 256, 256), 256)
            hot = onehot[rows, :]
            want = colb[rows, :]
            total = acc[rows, :]
            for ref, base in refs:
                found = jnp.dot(hot, ref[...], preferred_element_type=F32)
                total = total + jnp.where(want == base, found, 0.0)
            acc[rows, :] = total
            return 0

        lax.fori_loop(0, NG // 256, body, 0)

    for d in (1, 3, 2):
        copies["py", d].wait_recv()
        tile = pall.at[c, lay_of(-d)]
        for e in (1, 3, 2):
            part = tile.at[low]
            copies["a", d, e] = push(("a", d, e), part, part, {"col": col_of(2 * e)})
        copies["sy", d] = push(("sy", d), tile, tile, {"col": sib})
        copies["px", d].wait_recv()
        tile = pall.at[col_of(-2 * d), l]
        for e in (1, 3, 2):
            part = tile.at[high]
            copies["b", d, e] = push(("b", d, e), part, part, {"layer": lay_of(e)})
        copies["sx", d] = push(("sx", d), tile, tile, {"col": sib})

    ring(1)
    pos = lax.broadcasted_iota(jnp.int32, (EX, 128), 0)
    pos = jnp.where(pos < 20, pos, pos - 24).astype(F32)
    for k in range(NG // 128):
        rows = slice(k * 128, (k + 1) * 128)
        dz = pos_z - gcols[:, 16 + k : 17 + k]
        value = jnp.exp(-gcols[:, 24 + k : 25 + k] * dz * dz)
        ez[rows, :] = jnp.where(near_z & (jnp.abs(dz) <= R), value, 0.0)

    def make_plane(k, _):
        cols = pl.ds(pl.multiple_of(k * 128, 128), 128)
        at = g_int[2, pl.ds(k, 1), :]
        expo = g_float[0, pl.ds(k, 1), :]
        dx = pos - (at >> 11).astype(F32)
        ex = jnp.where(jnp.abs(dx) <= R, jnp.exp(-expo * dx * dx), 0.0)
        dy = pos - ((at >> 7) & (GY - 1)).astype(F32)
        ey = jnp.where(jnp.abs(dy) <= R, jnp.exp(-expo * dy * dy), 0.0)
        for i in range(0, EX, 2):
            value = jnp.concatenate([ex[i : i + 1, :] * ey, ex[i + 1 : i + 2, :] * ey], axis=0)
            upper = value.astype(BF16)
            plane_hi[i * EY : (i + 2) * EY, cols] = upper
            plane_lo[i * EY : (i + 2) * EY, cols] = (value - upper.astype(F32)).astype(BF16)
        return 0

    lax.fori_loop(0, NG // 128, make_plane, 0)
    lookup([(c, l)] + [(c, lay_of(-d)) for d in (1, 3, 2)] + [(col_of(-2 * d), l) for d in (1, 3, 2)])
    ring(2)

    copies["ps"].wait_recv()
    for d in (1, 3, 2):
        copies["sy", d].wait_recv()
        copies["sx", d].wait_recv()
    sib_of = lambda d: lax.rem(sib + (d + NC), NC)
    lookup([(sib, l)] + [(sib, lay_of(-d)) for d in (1, 3, 2)] + [(sib_of(-2 * d), l) for d in (1, 3, 2)])

    for d in (1, 3, 2):
        for e in (1, 3, 2):
            copies["a", d, e].wait_recv()
            part = pall.at[col_of(-2 * e), lay_of(-d), low]
            copies["sa", d, e] = push(("sa", d, e), part, part, {"col": sib})
            copies["b", d, e].wait_recv()
            part = pall.at[col_of(-2 * d), lay_of(-e), high]
            copies["sb", d, e] = push(("sb", d, e), part, part, {"col": sib})
    corners = [(d, e) for d in (1, 3, 2) for e in (1, 3, 2)]
    lookup([(col_of(-2 * d), lay_of(-e)) for d, e in corners])
    ring(3)
    for d, e in corners:
        copies["sa", d, e].wait_recv()
        copies["sb", d, e].wait_recv()
    lookup([(sib_of(-2 * d), lay_of(-e)) for d, e in corners])

    for k in range(NG // 128):
        rows = slice(k * 128, (k + 1) * 128)
        coef = jnp.sum(acc[rows, :], axis=1, keepdims=True) * gcols[:, 32 + k : 33 + k]
        ez[rows, :] = ez[rows, :] * coef

    depth = ez[...]
    depth_hi = depth.astype(BF16)
    depth_lo = (depth - depth_hi.astype(F32)).astype(BF16)
    step = 4 * EY
    for k in range(EX // 4):
        rows = slice(k * step, (k + 1) * step)
        part = jnp.dot(plane_hi[rows, :], depth_lo, preferred_element_type=F32)
        part = part + jnp.dot(plane_lo[rows, :], depth_hi, preferred_element_type=F32)
        part = part + jnp.dot(plane_hi[rows, :], depth_hi, preferred_element_type=F32)
        dens[k * 4 : (k + 1) * 4] = part[:, :128].reshape(4, EY, 128)
        gpad[rows, :] = part[:, 128:]
    gpad[EX * EY : 640, :] = jnp.zeros((64, 128), F32)
    for k in range(5):
        turned = jnp.transpose(gpad[k * 128 : (k + 1) * 128, :])
        rim[:, k * 128 : (k + 1) * 128] = turned[0:16, :]
    rim_in[8:120, :] = jnp.zeros((112, 640), F32)
    up = {"layer": lay_of(1)}
    down = {"layer": lay_of(-1)}
    copies["lu"] = push(("lu",), rim.at[0:8], rim_in.at[0:8], up)
    copies["ld"] = push(("ld",), rim.at[8:16], rim_in.at[120:128], down)
    ring(4)
    ring(5)

    copies["lu"].wait_recv()
    copies["ld"].wait_recv()
    for k in range(5):
        gpad[k * 128 : (k + 1) * 128, :] = jnp.transpose(rim_in[:, k * 128 : (k + 1) * 128])
    for k in range(EX):
        dens[k] = dens[k] + gpad[k * EY : (k + 1) * EY, :]
    copies["ru"] = push(("ru",), dens.at[16:20], row_in.at[0], right)
    copies["rd"] = push(("rd",), dens.at[20:24], row_in.at[1], left)
    ring(6)

    copies["ru"].wait_recv()
    copies["rd"].wait_recv()
    dens[0:4] = dens[0:4] + row_in[0]
    dens[12:16] = dens[12:16] + row_in[1]
    edge = dens.at[0:16, 16:24]
    copies["cu"] = push(("cu",), edge, col_in.at[0], {"col": col_of(1)})
    copies["cd"] = push(("cd",), edge, col_in.at[1], {"col": col_of(-1)})
    ring(7)
    ring(8)

    total = jnp.zeros((256, 128), F32)
    for b in range(NL):
        for k in range(NC // 2):
            lhs = jnp.concatenate([pall[2 * k, b], pall[2 * k + 1, b]], axis=1)
            rhs = hall[b, 4 * k : 4 * k + 4].reshape(256, 128)
            total = total + jnp.dot(lhs, rhs, preferred_element_type=F32)
    prod_ref[...] = total.astype(BF16)

    copies["cu"].wait_recv()
    copies["cd"].wait_recv()
    inner = lax.broadcasted_iota(jnp.int32, (16, 8, 128), 1)
    dens_ref[:, 0:8, :] = dens[0:16, 0:8, :] + jnp.where(inner < 4, col_in[0], 0.0)
    dens_ref[:, 8:16, :] = dens[0:16, 8:16, :] + jnp.where(inner >= 4, col_in[1], 0.0)
    for copy in pending:
        copy.wait_send()


def on_device(
    p_slabs, p_mask, h_slabs, h_mask, gauss_row, gauss_col, gauss_cell, gauss_expo, gauss_pref
):
    n_sem = 128
    vmem = pl.BlockSpec(memory_space=pltpu.VMEM)
    return pl.pallas_call(
        kernel,
        out_shape=(
            jax.ShapeDtypeStruct((256, 128), BF16),
            jax.ShapeDtypeStruct((GX, GY, GZ), F32),
        ),
        in_specs=[pl.BlockSpec(memory_space=pl.ANY)] * 9,
        out_specs=(vmem, vmem),
        scratch_shapes=[
            pltpu.VMEM((256, 128), BF16),
            pltpu.VMEM((4, 8), jnp.int32),
            pltpu.VMEM((64, 512), BF16),
            pltpu.VMEM((2, 16), jnp.int32),
            pltpu.VMEM((3, 8, 128), jnp.int32),
            pltpu.VMEM((2, 8, 128), F32),
            pltpu.VMEM((NL, 64, 128), BF16),
            pltpu.VMEM((128, 128), F32),
            pltpu.VMEM((NC, NL, 256, 128), BF16),
            pltpu.VMEM((NL, NR, 64, 128), BF16),
            pltpu.VMEM((640, 128), F32),
            pltpu.VMEM((128, 128), F32),
            pltpu.VMEM((NG, 256), BF16),
            pltpu.VMEM((NG, 128), F32),
            pltpu.VMEM((NG, 128), F32),
            pltpu.VMEM((NG, 256), F32),
            pltpu.VMEM((EX * EY, NG), BF16),
            pltpu.VMEM((EX * EY, NG), BF16),
            pltpu.VMEM((EX, EY, 128), F32),
            pltpu.VMEM((16, 640), F32),
            pltpu.VMEM((128, 640), F32),
            pltpu.VMEM((2, 4, EY, 128), F32),
            pltpu.VMEM((2, 16, 8, 128), F32),
            pltpu.SemaphoreType.DMA((n_sem,)),
            pltpu.SemaphoreType.DMA((n_sem,)),
            pltpu.SemaphoreType.DMA((11,)),
        ],
        compiler_params=pltpu.CompilerParams(collective_id=0, has_side_effects=True),
    )(
        p_slabs[0], jnp.transpose(p_mask[0]), h_slabs[0], h_mask[0],
        gauss_row.reshape(8, 128), gauss_col.reshape(8, 128), gauss_cell.reshape(8, 128),
        gauss_expo.reshape(8, 128), gauss_pref.reshape(8, 128),
    )


def solution(mesh):
    placed = (
        P("layer", "row", "col"),
        P("layer", "row", "col"),
        P("layer", "row", "col"),
        P("layer", "row", "col"),
        P(("row", "col", "layer")),
        P(("row", "col", "layer")),
        P(("row", "col", "layer")),
        P(("row", "col", "layer")),
        P(("row", "col", "layer")),
    )
    return jax.shard_map(
        on_device,
        mesh=mesh,
        in_specs=placed,
        out_specs=(P("row", ("col", "layer")), P("row", "col", "layer")),
        check_vma=False,
    )
```

```python
import jax
import jax.numpy as jnp
from jax import lax
from jax.experimental import pallas as pl
from jax.experimental.pallas import tpu as pltpu
from jax.sharding import PartitionSpec as P

BS = 32
GX = 16
GY = 16
GZ = 128
R = 4
NG = 1024
NR = 16
NC = 8
NL = 4
EX = GX + 2 * R
EY = GY + 2 * R
F32 = jnp.float32
BF16 = jnp.bfloat16


def kernel(
    p_hbm, pm_hbm, h_hbm, hm_hbm, row_hbm, gcol_hbm, cell_hbm, expo_hbm, pref_hbm, prod_ref, dens_ref,
    p_in, pm_in, h_in, hm_in, g_int, g_float, h_ref, turn, pall, hall, gpad, gcols, onehot, colb, acc, ez, plane_hi, plane_lo, dens, rim, rim_in, row_in, col_in,
    send, recv, local,
):
    r = lax.axis_index("row")
    c = lax.axis_index("col")
    l = lax.axis_index("layer")
    row_of = lambda d: lax.rem(r + (d + NR), NR)
    col_of = lambda d: lax.rem(c + (d + NC), NC)
    lay_of = lambda d: lax.rem(l + (d + NL), NL)
    odd = lax.rem(c, 2)
    sib = c + 1 - 2 * odd
    out = c - 1 + 2 * odd
    other = lax.rem(out + NC, NC)

    loads = [
        pltpu.make_async_copy(src, dst, local.at[2 + n])
        for n, (src, dst) in enumerate(
            [(p_hbm, p_in), (pm_hbm, pm_in), (h_hbm, h_in), (hm_hbm, hm_in), (row_hbm, g_int.at[0]), (gcol_hbm, g_int.at[1]),
             (cell_hbm, g_int.at[2]), (expo_hbm, g_float.at[0]), (pref_hbm, g_float.at[1])]
        )
    ]
    for copy in loads:
        copy.start()
    barrier = pltpu.get_barrier_semaphore()
    peers = (
        [{"layer": lay_of(d)} for d in (1, 2, 3)]
        + [{"col": col_of(2 * d)} for d in (1, 2, 3)]
        + [{"col": sib}, {"col": other}]
        + [{"row": row_of(d)} for d in (1, -1, 2, -2)]
    )
    for peer in peers:
        pl.semaphore_signal(barrier, inc=1, device_id=peer, device_id_type=pl.DeviceIdType.MESH)
    block = lax.broadcasted_iota(jnp.int32, (4, 128), 0)
    of_lane = lax.broadcasted_iota(jnp.int32, (4, 128), 1) // BS
    loads[0].wait()
    loads[1].wait()
    for i in range(256 // BS):
        column = jnp.broadcast_to(pm_in[:, i : i + 1], (4, 128))
        keep = jnp.sum(jnp.where(block == of_lane, column, 0), axis=0, keepdims=True) > 0
        rows = slice(i * BS, (i + 1) * BS)
        value = jnp.where(jnp.broadcast_to(keep, (BS, 128)), p_in[rows, :].astype(F32), 0.0)
        pall[c, l, rows, :] = value.astype(BF16)
    loads[2].wait()
    loads[3].wait()
    of_lane = lax.broadcasted_iota(jnp.int32, (1, 128), 1) // BS
    for q in range(NL):
        for i in range(64 // BS):
            keep = jnp.zeros((1, 128), jnp.int32)
            for j in range(4):
                at = q * 4 + j
                keep = jnp.where(of_lane == j, jnp.broadcast_to(hm_in[i : i + 1, at : at + 1], (1, 128)), keep)
            rows = slice(i * BS, (i + 1) * BS)
            value = h_in[rows, q * 128 : (q + 1) * 128].astype(F32)
            value = jnp.where(jnp.broadcast_to(keep > 0, (BS, 128)), value, 0.0)
            h_ref[q, rows, :] = value.astype(BF16)
    own_h = pltpu.make_async_copy(h_ref.at[l], hall.at[l, r], local.at[1])
    own_h.start()
    p_ref = pall.at[c, l]
    pl.semaphore_wait(barrier, len(peers))

    pending = []
    slots = {}

    def push(key, src, dst, peer):
        n = slots.setdefault(key, len(slots))
        copy = pltpu.make_async_remote_copy(
            src_ref=src, dst_ref=dst, send_sem=send.at[n], recv_sem=recv.at[n],
            device_id=peer, device_id_type=pl.DeviceIdType.MESH,
        )
        copy.start()
        pending.append(copy)
        return copy

    low = pl.ds(0, 128)
    high = pl.ds(128, 128)
    copies = {}
    right = {"row": row_of(1)}
    left = {"row": row_of(-1)}
    order = (0, 1, 3, 2)
    tree = [
        (0, 2), (0, -2), (0, 1), (0, -1), (2, 4), (-2, -4), (2, 3), (-2, -3),
        (4, 6), (-4, -6), (4, 5), (-4, -5), (6, 8), (6, 7), (-6, -7),
    ]

    def spread(parent, d):
        if parent:
            copies["h", parent, d].wait_recv()
        for source, target in tree:
            if source == parent:
                piece = hall.at[lay_of(-d), row_of(-parent)]
                peer = {"row": row_of(target - parent)}
                copies["h", target, d] = push(("h", target, d), piece, piece, peer)

    def hop(parent):
        for d in order:
            spread(parent, d)
            spread(-parent, d)

    for d in (1, 3, 2):
        copies["ha", d] = push(("ha", d), h_ref.at[lay_of(d)], hall.at[l, r], {"layer": lay_of(d)})
    own_h.wait()
    spread(0, 0)
    for d in (1, 3, 2):
        copies["py", d] = push(("py", d), p_ref, pall.at[c, l], {"layer": lay_of(d)})
        copies["px", d] = push(("px", d), p_ref, pall.at[c, l], {"col": col_of(2 * d)})
    copies["ps"] = push(("ps",), p_ref, pall.at[c, l], {"col": sib})

    for copy in loads[4:]:
        copy.wait()
    cell = g_int[2]
    turn[0:8, :] = g_int[0].astype(F32)
    turn[8:16, :] = g_int[1].astype(F32)
    turn[16:24, :] = (cell & (GZ - 1)).astype(F32)
    turn[24:32, :] = g_float[0]
    turn[32:40, :] = g_float[1]
    turn[40:128, :] = jnp.zeros((88, 128), F32)
    gcols[...] = jnp.transpose(turn[...])

    for d in order[1:]:
        copies["ha", d].wait_recv()
        spread(0, d)
    lane = lax.broadcasted_iota(jnp.int32, (128, 256), 1)
    lane_f = lane.astype(F32)
    pos_z = jnp.where(lane < 136, lane, lane - 144).astype(F32)
    near_z = (lane < 132) | ((lane >= 140) & (lane < 144))
    for k in range(NG // 128):
        rows = slice(k * 128, (k + 1) * 128)
        onehot[rows, :] = jnp.where(gcols[:, k : k + 1] == lane_f, 1.0, 0.0).astype(BF16)
        colb[rows, :] = gcols[:, 8 + k : 9 + k] - lane_f[:, :128]
        acc[rows, :] = jnp.zeros((128, 128), F32)

    def lookup(tiles):
        refs = [(pall.at[a, b], (b * NG + a * 128).astype(F32)) for a, b in tiles]

        def body(k, _):
            rows = pl.ds(pl.multiple_of(k * 256, 256), 256)
            hot = onehot[rows, :]
            want = colb[rows, :]
            total = acc[rows, :]
            for ref, base in refs:
                found = jnp.dot(hot, ref[...], preferred_element_type=F32)
                total = total + jnp.where(want == base, found, 0.0)
            acc[rows, :] = total
            return 0

        lax.fori_loop(0, NG // 256, body, 0)

    for d in (1, 3, 2):
        copies["py", d].wait_recv()
        tile = pall.at[c, lay_of(-d)]
        for e in (1, 3, 2):
            part = tile.at[low]
            copies["a", d, e] = push(("a", d, e), part, part, {"col": col_of(2 * e)})
        copies["sy", d] = push(("sy", d), tile, tile, {"col": sib})
        copies["px", d].wait_recv()
        tile = pall.at[col_of(-2 * d), l]
        for e in (1, 3, 2):
            part = tile.at[high]
            copies["b", d, e] = push(("b", d, e), part, part, {"layer": lay_of(e)})
        copies["sx", d] = push(("sx", d), tile, tile, {"col": sib})

    pos = lax.broadcasted_iota(jnp.int32, (EX, 128), 0)
    pos = jnp.where(pos < 20, pos, pos - 24).astype(F32)
    for k in range(NG // 128):
        rows = slice(k * 128, (k + 1) * 128)
        dz = pos_z - gcols[:, 16 + k : 17 + k]
        value = jnp.exp(-gcols[:, 24 + k : 25 + k] * dz * dz)
        ez[rows, :] = jnp.where(near_z & (jnp.abs(dz) <= R), value, 0.0)

    def make_plane(k, _):
        cols = pl.ds(pl.multiple_of(k * 128, 128), 128)
        at = g_int[2, pl.ds(k, 1), :]
        expo = g_float[0, pl.ds(k, 1), :]
        dx = pos - (at >> 11).astype(F32)
        ex = jnp.where(jnp.abs(dx) <= R, jnp.exp(-expo * dx * dx), 0.0)
        dy = pos - ((at >> 7) & (GY - 1)).astype(F32)
        ey = jnp.where(jnp.abs(dy) <= R, jnp.exp(-expo * dy * dy), 0.0)
        for i in range(0, EX, 2):
            value = jnp.concatenate([ex[i : i + 1, :] * ey, ex[i + 1 : i + 2, :] * ey], axis=0)
            upper = value.astype(BF16)
            plane_hi[i * EY : (i + 2) * EY, cols] = upper
            plane_lo[i * EY : (i + 2) * EY, cols] = (value - upper.astype(F32)).astype(BF16)
        return 0

    lax.fori_loop(0, NG // 128, make_plane, 0)
    lookup([(c, l)] + [(c, lay_of(-d)) for d in (1, 3, 2)] + [(col_of(-2 * d), l) for d in (1, 3, 2)])
    hop(2)

    copies["ps"].wait_recv()
    for d in (1, 3, 2):
        copies["sy", d].wait_recv()
        copies["sx", d].wait_recv()
    sib_of = lambda d: lax.rem(sib + (d + NC), NC)
    lookup([(sib, l)] + [(sib, lay_of(-d)) for d in (1, 3, 2)] + [(sib_of(-2 * d), l) for d in (1, 3, 2)])

    for d in (1, 3, 2):
        for e in (1, 3, 2):
            copies["a", d, e].wait_recv()
            part = pall.at[col_of(-2 * e), lay_of(-d), low]
            copies["sa", d, e] = push(("sa", d, e), part, part, {"col": sib})
            copies["b", d, e].wait_recv()
            part = pall.at[col_of(-2 * d), lay_of(-e), high]
            copies["sb", d, e] = push(("sb", d, e), part, part, {"col": sib})
    corners = [(d, e) for d in (1, 3, 2) for e in (1, 3, 2)]
    lookup([(col_of(-2 * d), lay_of(-e)) for d, e in corners])
    hop(4)
    for d, e in corners:
        copies["sa", d, e].wait_recv()
        copies["sb", d, e].wait_recv()
    lookup([(sib_of(-2 * d), lay_of(-e)) for d, e in corners])

    for k in range(NG // 128):
        rows = slice(k * 128, (k + 1) * 128)
        coef = jnp.sum(acc[rows, :], axis=1, keepdims=True) * gcols[:, 32 + k : 33 + k]
        ez[rows, :] = ez[rows, :] * coef

    depth = ez[...]
    depth_hi = depth.astype(BF16)
    depth_lo = (depth - depth_hi.astype(F32)).astype(BF16)
    step = 4 * EY
    for k in range(EX // 4):
        rows = slice(k * step, (k + 1) * step)
        part = jnp.dot(plane_hi[rows, :], depth_lo, preferred_element_type=F32)
        part = part + jnp.dot(plane_lo[rows, :], depth_hi, preferred_element_type=F32)
        part = part + jnp.dot(plane_hi[rows, :], depth_hi, preferred_element_type=F32)
        dens[k * 4 : (k + 1) * 4] = part[:, :128].reshape(4, EY, 128)
        gpad[rows, :] = part[:, 128:]
    gpad[EX * EY : 640, :] = jnp.zeros((64, 128), F32)
    for k in range(5):
        turned = jnp.transpose(gpad[k * 128 : (k + 1) * 128, :])
        rim[:, k * 128 : (k + 1) * 128] = turned[0:16, :]
    rim_in[8:120, :] = jnp.zeros((112, 640), F32)
    up = {"layer": lay_of(1)}
    down = {"layer": lay_of(-1)}
    copies["lu"] = push(("lu",), rim.at[0:8], rim_in.at[0:8], up)
    copies["ld"] = push(("ld",), rim.at[8:16], rim_in.at[120:128], down)

    copies["lu"].wait_recv()
    copies["ld"].wait_recv()
    for k in range(5):
        gpad[k * 128 : (k + 1) * 128, :] = jnp.transpose(rim_in[:, k * 128 : (k + 1) * 128])
    for k in range(EX):
        dens[k] = dens[k] + gpad[k * EY : (k + 1) * EY, :]
    copies["ru"] = push(("ru",), dens.at[16:20], row_in.at[0], right)
    copies["rd"] = push(("rd",), dens.at[20:24], row_in.at[1], left)
    hop(6)

    copies["ru"].wait_recv()
    copies["rd"].wait_recv()
    dens[0:4] = dens[0:4] + row_in[0]
    dens[12:16] = dens[12:16] + row_in[1]
    edge = dens.at[0:16, 16:24]
    copies["cu"] = push(("cu",), edge, col_in.at[0], {"col": col_of(1)})
    copies["cd"] = push(("cd",), edge, col_in.at[1], {"col": col_of(-1)})
    for leaf in (1, -1, 3, -3, 5, -5, 7, -7, 8):
        for d in order:
            copies["h", leaf, d].wait_recv()

    total = jnp.zeros((256, 128), F32)
    for b in range(NL):
        for k in range(NC // 2):
            lhs = jnp.concatenate([pall[2 * k, b], pall[2 * k + 1, b]], axis=1)
            rhs = hall[b, 4 * k : 4 * k + 4].reshape(256, 128)
            total = total + jnp.dot(lhs, rhs, preferred_element_type=F32)
    prod_ref[...] = total.astype(BF16)

    copies["cu"].wait_recv()
    copies["cd"].wait_recv()
    inner = lax.broadcasted_iota(jnp.int32, (16, 8, 128), 1)
    dens_ref[:, 0:8, :] = dens[0:16, 0:8, :] + jnp.where(inner < 4, col_in[0], 0.0)
    dens_ref[:, 8:16, :] = dens[0:16, 8:16, :] + jnp.where(inner >= 4, col_in[1], 0.0)
    for copy in pending:
        copy.wait_send()


def on_device(
    p_slabs, p_mask, h_slabs, h_mask, gauss_row, gauss_col, gauss_cell, gauss_expo, gauss_pref
):
    n_sem = 128
    vmem = pl.BlockSpec(memory_space=pltpu.VMEM)
    return pl.pallas_call(
        kernel,
        out_shape=(
            jax.ShapeDtypeStruct((256, 128), BF16),
            jax.ShapeDtypeStruct((GX, GY, GZ), F32),
        ),
        in_specs=[pl.BlockSpec(memory_space=pl.ANY)] * 9,
        out_specs=(vmem, vmem),
        scratch_shapes=[
            pltpu.VMEM((256, 128), BF16),
            pltpu.VMEM((4, 8), jnp.int32),
            pltpu.VMEM((64, 512), BF16),
            pltpu.VMEM((2, 16), jnp.int32),
            pltpu.VMEM((3, 8, 128), jnp.int32),
            pltpu.VMEM((2, 8, 128), F32),
            pltpu.VMEM((NL, 64, 128), BF16),
            pltpu.VMEM((128, 128), F32),
            pltpu.VMEM((NC, NL, 256, 128), BF16),
            pltpu.VMEM((NL, NR, 64, 128), BF16),
            pltpu.VMEM((640, 128), F32),
            pltpu.VMEM((128, 128), F32),
            pltpu.VMEM((NG, 256), BF16),
            pltpu.VMEM((NG, 128), F32),
            pltpu.VMEM((NG, 128), F32),
            pltpu.VMEM((NG, 256), F32),
            pltpu.VMEM((EX * EY, NG), BF16),
            pltpu.VMEM((EX * EY, NG), BF16),
            pltpu.VMEM((EX, EY, 128), F32),
            pltpu.VMEM((16, 640), F32),
            pltpu.VMEM((128, 640), F32),
            pltpu.VMEM((2, 4, EY, 128), F32),
            pltpu.VMEM((2, 16, 8, 128), F32),
            pltpu.SemaphoreType.DMA((n_sem,)),
            pltpu.SemaphoreType.DMA((n_sem,)),
            pltpu.SemaphoreType.DMA((11,)),
        ],
        compiler_params=pltpu.CompilerParams(collective_id=0, has_side_effects=True),
    )(
        p_slabs[0], jnp.transpose(p_mask[0]), h_slabs[0], h_mask[0],
        gauss_row.reshape(8, 128), gauss_col.reshape(8, 128), gauss_cell.reshape(8, 128),
        gauss_expo.reshape(8, 128), gauss_pref.reshape(8, 128),
    )


def solution(mesh):
    placed = (
        P("layer", "row", "col"),
        P("layer", "row", "col"),
        P("layer", "row", "col"),
        P("layer", "row", "col"),
        P(("row", "col", "layer")),
        P(("row", "col", "layer")),
        P(("row", "col", "layer")),
        P(("row", "col", "layer")),
        P(("row", "col", "layer")),
    )
    return jax.shard_map(
        on_device,
        mesh=mesh,
        in_specs=placed,
        out_specs=(P("row", ("col", "layer")), P("row", "col", "layer")),
        check_vma=False,
    )
```

```python
import jax
import jax.numpy as jnp
from jax import lax
from jax.experimental import pallas as pl
from jax.experimental.pallas import tpu as pltpu
from jax.sharding import PartitionSpec as P

BS = 32
GX = 16
GY = 16
GZ = 128
R = 4
NG = 1024
NR = 16
NC = 8
NL = 4
EX = GX + 2 * R
EY = GY + 2 * R
F32 = jnp.float32
BF16 = jnp.bfloat16


def kernel(
    p_hbm, pm_hbm, h_hbm, hm_hbm, row_hbm, gcol_hbm, cell_hbm, expo_hbm, pref_hbm, prod_ref, dens_ref,
    p_in, pm_in, h_in, hm_in, g_int, g_float, h_ref, turn, pall, hall, gpad, gcols, onehot, colb, acc, ez, plane_hi, plane_lo, dens, rim, rim_in, row_in, col_in, side_in,
    send, recv, local,
):
    r = lax.axis_index("row")
    c = lax.axis_index("col")
    l = lax.axis_index("layer")
    row_of = lambda d: lax.rem(r + (d + NR), NR)
    col_of = lambda d: lax.rem(c + (d + NC), NC)
    lay_of = lambda d: lax.rem(l + (d + NL), NL)
    odd = lax.rem(c, 2)
    sib = c + 1 - 2 * odd
    out = c - 1 + 2 * odd
    other = lax.rem(out + NC, NC)

    loads = [
        pltpu.make_async_copy(src, dst, local.at[2 + n])
        for n, (src, dst) in enumerate(
            [(p_hbm, p_in), (pm_hbm, pm_in), (h_hbm, h_in), (hm_hbm, hm_in), (row_hbm, g_int.at[0]), (gcol_hbm, g_int.at[1]),
             (cell_hbm, g_int.at[2]), (expo_hbm, g_float.at[0]), (pref_hbm, g_float.at[1])]
        )
    ]
    for copy in loads:
        copy.start()
    barrier = pltpu.get_barrier_semaphore()
    peers = (
        [{"layer": lay_of(d)} for d in (1, 2, 3)]
        + [{"col": col_of(2 * d)} for d in (1, 2, 3)]
        + [{"col": sib}, {"col": other}]
        + [{"row": row_of(d)} for d in (1, -1, 2, -2)]
        + [{"row": row_of(a), "layer": lay_of(b)} for a in (1, -1) for b in (1, -1)]
    )
    for peer in peers:
        pl.semaphore_signal(barrier, inc=1, device_id=peer, device_id_type=pl.DeviceIdType.MESH)
    block = lax.broadcasted_iota(jnp.int32, (4, 128), 0)
    of_lane = lax.broadcasted_iota(jnp.int32, (4, 128), 1) // BS
    loads[0].wait()
    loads[1].wait()
    for i in range(256 // BS):
        column = jnp.broadcast_to(pm_in[:, i : i + 1], (4, 128))
        keep = jnp.sum(jnp.where(block == of_lane, column, 0), axis=0, keepdims=True) > 0
        rows = slice(i * BS, (i + 1) * BS)
        value = jnp.where(jnp.broadcast_to(keep, (BS, 128)), p_in[rows, :].astype(F32), 0.0)
        pall[c, l, rows, :] = value.astype(BF16)
    loads[2].wait()
    loads[3].wait()
    of_lane = lax.broadcasted_iota(jnp.int32, (1, 128), 1) // BS
    for q in range(NL):
        for i in range(64 // BS):
            keep = jnp.zeros((1, 128), jnp.int32)
            for j in range(4):
                at = q * 4 + j
                keep = jnp.where(of_lane == j, jnp.broadcast_to(hm_in[i : i + 1, at : at + 1], (1, 128)), keep)
            rows = slice(i * BS, (i + 1) * BS)
            value = h_in[rows, q * 128 : (q + 1) * 128].astype(F32)
            value = jnp.where(jnp.broadcast_to(keep > 0, (BS, 128)), value, 0.0)
            h_ref[q, rows, :] = value.astype(BF16)
    own_h = pltpu.make_async_copy(h_ref.at[l], hall.at[l, r], local.at[1])
    own_h.start()
    p_ref = pall.at[c, l]
    pl.semaphore_wait(barrier, len(peers))

    pending = []
    slots = {}

    def push(key, src, dst, peer):
        n = slots.setdefault(key, len(slots))
        copy = pltpu.make_async_remote_copy(
            src_ref=src, dst_ref=dst, send_sem=send.at[n], recv_sem=recv.at[n],
            device_id=peer, device_id_type=pl.DeviceIdType.MESH,
        )
        copy.start()
        pending.append(copy)
        return copy

    low = pl.ds(0, 128)
    high = pl.ds(128, 128)
    copies = {}
    right = {"row": row_of(1)}
    left = {"row": row_of(-1)}
    order = (0, 1, 3, 2)
    tree = [
        (0, 2), (0, -2), (0, 1), (0, -1), (2, 4), (-2, -4), (2, 3), (-2, -3),
        (4, 6), (-4, -6), (4, 5), (-4, -5), (6, 8), (6, 7), (-6, -7),
    ]

    def spread(parent, d):
        if parent:
            copies["h", parent, d].wait_recv()
        for source, target in tree:
            if source == parent:
                piece = hall.at[lay_of(-d), row_of(-parent)]
                peer = {"row": row_of(target - parent)}
                copies["h", target, d] = push(("h", target, d), piece, piece, peer)

    def hop(parent):
        for d in order:
            spread(parent, d)
            spread(-parent, d)

    for d in (1, 3, 2):
        copies["ha", d] = push(("ha", d), h_ref.at[lay_of(d)], hall.at[l, r], {"layer": lay_of(d)})
    own_h.wait()
    spread(0, 0)
    for d in (1, 3, 2):
        copies["py", d] = push(("py", d), p_ref, pall.at[c, l], {"layer": lay_of(d)})
        copies["px", d] = push(("px", d), p_ref, pall.at[c, l], {"col": col_of(2 * d)})
    copies["ps"] = push(("ps",), p_ref, pall.at[c, l], {"col": sib})

    for copy in loads[4:]:
        copy.wait()
    cell = g_int[2]
    turn[0:8, :] = g_int[0].astype(F32)
    turn[8:16, :] = g_int[1].astype(F32)
    turn[16:24, :] = (cell & (GZ - 1)).astype(F32)
    turn[24:32, :] = g_float[0]
    turn[32:40, :] = g_float[1]
    turn[40:128, :] = jnp.zeros((88, 128), F32)
    gcols[...] = jnp.transpose(turn[...])

    for d in order[1:]:
        copies["ha", d].wait_recv()
        spread(0, d)
    lane = lax.broadcasted_iota(jnp.int32, (128, 256), 1)
    lane_f = lane.astype(F32)
    pos_z = jnp.where(lane < 136, lane, lane - 144).astype(F32)
    near_z = (lane < 132) | ((lane >= 140) & (lane < 144))
    for k in range(NG // 128):
        rows = slice(k * 128, (k + 1) * 128)
        onehot[rows, :] = jnp.where(gcols[:, k : k + 1] == lane_f, 1.0, 0.0).astype(BF16)
        colb[rows, :] = gcols[:, 8 + k : 9 + k] - lane_f[:, :128]
        acc[rows, :] = jnp.zeros((128, 128), F32)

    def lookup(tiles):
        refs = [(pall.at[a, b], (b * NG + a * 128).astype(F32)) for a, b in tiles]

        def body(k, _):
            rows = pl.ds(pl.multiple_of(k * 256, 256), 256)
            hot = onehot[rows, :]
            want = colb[rows, :]
            total = acc[rows, :]
            for ref, base in refs:
                found = jnp.dot(hot, ref[...], preferred_element_type=F32)
                total = total + jnp.where(want == base, found, 0.0)
            acc[rows, :] = total
            return 0

        lax.fori_loop(0, NG // 256, body, 0)

    for d in (1, 3, 2):
        copies["py", d].wait_recv()
        tile = pall.at[c, lay_of(-d)]
        for e in (1, 3, 2):
            part = tile.at[low]
            copies["a", d, e] = push(("a", d, e), part, part, {"col": col_of(2 * e)})
        copies["sy", d] = push(("sy", d), tile, tile, {"col": sib})
        copies["px", d].wait_recv()
        tile = pall.at[col_of(-2 * d), l]
        for e in (1, 3, 2):
            part = tile.at[high]
            copies["b", d, e] = push(("b", d, e), part, part, {"layer": lay_of(e)})
        copies["sx", d] = push(("sx", d), tile, tile, {"col": sib})

    pos = lax.broadcasted_iota(jnp.int32, (EX, 128), 0)
    pos = jnp.where(pos < 20, pos, pos - 24).astype(F32)
    for k in range(NG // 128):
        rows = slice(k * 128, (k + 1) * 128)
        dz = pos_z - gcols[:, 16 + k : 17 + k]
        value = jnp.exp(-gcols[:, 24 + k : 25 + k] * dz * dz)
        ez[rows, :] = jnp.where(near_z & (jnp.abs(dz) <= R), value, 0.0)

    def make_plane(k, _):
        cols = pl.ds(pl.multiple_of(k * 128, 128), 128)
        at = g_int[2, pl.ds(k, 1), :]
        expo = g_float[0, pl.ds(k, 1), :]
        dx = pos - (at >> 11).astype(F32)
        ex = jnp.where(jnp.abs(dx) <= R, jnp.exp(-expo * dx * dx), 0.0)
        dy = pos - ((at >> 7) & (GY - 1)).astype(F32)
        ey = jnp.where(jnp.abs(dy) <= R, jnp.exp(-expo * dy * dy), 0.0)
        for i in range(0, EX, 2):
            value = jnp.concatenate([ex[i : i + 1, :] * ey, ex[i + 1 : i + 2, :] * ey], axis=0)
            upper = value.astype(BF16)
            plane_hi[i * EY : (i + 2) * EY, cols] = upper
            plane_lo[i * EY : (i + 2) * EY, cols] = (value - upper.astype(F32)).astype(BF16)
        return 0

    lax.fori_loop(0, NG // 128, make_plane, 0)
    lookup([(c, l)] + [(c, lay_of(-d)) for d in (1, 3, 2)] + [(col_of(-2 * d), l) for d in (1, 3, 2)])
    hop(2)

    copies["ps"].wait_recv()
    for d in (1, 3, 2):
        copies["sy", d].wait_recv()
        copies["sx", d].wait_recv()
    sib_of = lambda d: lax.rem(sib + (d + NC), NC)
    lookup([(sib, l)] + [(sib, lay_of(-d)) for d in (1, 3, 2)] + [(sib_of(-2 * d), l) for d in (1, 3, 2)])

    for d in (1, 3, 2):
        for e in (1, 3, 2):
            copies["a", d, e].wait_recv()
            part = pall.at[col_of(-2 * e), lay_of(-d), low]
            copies["sa", d, e] = push(("sa", d, e), part, part, {"col": sib})
            copies["b", d, e].wait_recv()
            part = pall.at[col_of(-2 * d), lay_of(-e), high]
            copies["sb", d, e] = push(("sb", d, e), part, part, {"col": sib})
    corners = [(d, e) for d in (1, 3, 2) for e in (1, 3, 2)]
    lookup([(col_of(-2 * d), lay_of(-e)) for d, e in corners])
    hop(4)
    for d, e in corners:
        copies["sa", d, e].wait_recv()
        copies["sb", d, e].wait_recv()
    lookup([(sib_of(-2 * d), lay_of(-e)) for d, e in corners])

    for k in range(NG // 128):
        rows = slice(k * 128, (k + 1) * 128)
        coef = jnp.sum(acc[rows, :], axis=1, keepdims=True) * gcols[:, 32 + k : 33 + k]
        ez[rows, :] = ez[rows, :] * coef

    depth = ez[...]
    depth_hi = depth.astype(BF16)
    depth_lo = (depth - depth_hi.astype(F32)).astype(BF16)
    step = 4 * EY
    for k in range(EX // 4):
        rows = slice(k * step, (k + 1) * step)
        part = jnp.dot(plane_hi[rows, :], depth_lo, preferred_element_type=F32)
        part = part + jnp.dot(plane_lo[rows, :], depth_hi, preferred_element_type=F32)
        part = part + jnp.dot(plane_hi[rows, :], depth_hi, preferred_element_type=F32)
        dens[k * 4 : (k + 1) * 4] = part[:, :128].reshape(4, EY, 128)
        gpad[rows, :] = part[:, 128:]
    gpad[EX * EY : 640, :] = jnp.zeros((64, 128), F32)
    for k in range(5):
        turned = jnp.transpose(gpad[k * 128 : (k + 1) * 128, :])
        rim[:, k * 128 : (k + 1) * 128] = turned[0:16, :]
    for n in range(2):
        side_in[n, 8:120, :] = jnp.zeros((112, 256), F32)
    rim_in[8:120, :] = jnp.zeros((112, 384), F32)
    up = {"layer": lay_of(1)}
    down = {"layer": lay_of(-1)}
    copies["ru"] = push(("ru",), dens.at[16:20], row_in.at[0], right)
    copies["rd"] = push(("rd",), dens.at[20:24], row_in.at[1], left)
    copies["lu"] = push(("lu",), rim.at[0:8, 0:384], rim_in.at[0:8], up)
    copies["ld"] = push(("ld",), rim.at[8:16, 0:384], rim_in.at[120:128], down)
    for n, step in enumerate((1, -1)):
        for name, dz, rows, into in (("u", 1, slice(0, 8), slice(0, 8)), ("d", -1, slice(8, 16), slice(120, 128))):
            peer = {"row": row_of(step), "layer": lay_of(dz)}
            copies["s", n, name] = push(("s", n, name), rim.at[rows, 384:640], side_in.at[n, into], peer)
    hop(6)

    for k in ("ru", "rd", "lu", "ld"):
        copies[k].wait_recv()
    for k in range(3):
        gpad[k * 128 : (k + 1) * 128, :] = jnp.transpose(rim_in[:, k * 128 : (k + 1) * 128])
    for k in range(GX):
        dens[k] = dens[k] + gpad[k * EY : (k + 1) * EY, :]
    for n, at in ((0, 0), (1, 12)):
        copies["s", n, "u"].wait_recv()
        copies["s", n, "d"].wait_recv()
        for k in range(2):
            gpad[384 + k * 128 : 512 + k * 128, :] = jnp.transpose(side_in[n, :, k * 128 : (k + 1) * 128])
        for k in range(4):
            here = 384 + (n * 4 + k) * EY
            dens[at + k] = dens[at + k] + gpad[here : here + EY, :]
    dens[0:4] = dens[0:4] + row_in[0]
    dens[12:16] = dens[12:16] + row_in[1]
    edge = dens.at[0:16, 16:24]
    copies["cu"] = push(("cu",), edge, col_in.at[0], {"col": col_of(1)})
    copies["cd"] = push(("cd",), edge, col_in.at[1], {"col": col_of(-1)})
    for leaf in (1, -1, 3, -3, 5, -5, 7, -7, 8):
        for d in order:
            copies["h", leaf, d].wait_recv()

    total = jnp.zeros((256, 128), F32)
    for b in range(NL):
        for k in range(NC // 2):
            lhs = jnp.concatenate([pall[2 * k, b], pall[2 * k + 1, b]], axis=1)
            rhs = hall[b, 4 * k : 4 * k + 4].reshape(256, 128)
            total = total + jnp.dot(lhs, rhs, preferred_element_type=F32)
    prod_ref[...] = total.astype(BF16)

    copies["cu"].wait_recv()
    copies["cd"].wait_recv()
    inner = lax.broadcasted_iota(jnp.int32, (16, 8, 128), 1)
    dens_ref[:, 0:8, :] = dens[0:16, 0:8, :] + jnp.where(inner < 4, col_in[0], 0.0)
    dens_ref[:, 8:16, :] = dens[0:16, 8:16, :] + jnp.where(inner >= 4, col_in[1], 0.0)
    for copy in pending:
        copy.wait_send()


def on_device(
    p_slabs, p_mask, h_slabs, h_mask, gauss_row, gauss_col, gauss_cell, gauss_expo, gauss_pref
):
    n_sem = 128
    vmem = pl.BlockSpec(memory_space=pltpu.VMEM)
    return pl.pallas_call(
        kernel,
        out_shape=(
            jax.ShapeDtypeStruct((256, 128), BF16),
            jax.ShapeDtypeStruct((GX, GY, GZ), F32),
        ),
        in_specs=[pl.BlockSpec(memory_space=pl.ANY)] * 9,
        out_specs=(vmem, vmem),
        scratch_shapes=[
            pltpu.VMEM((256, 128), BF16),
            pltpu.VMEM((4, 8), jnp.int32),
            pltpu.VMEM((64, 512), BF16),
            pltpu.VMEM((2, 16), jnp.int32),
            pltpu.VMEM((3, 8, 128), jnp.int32),
            pltpu.VMEM((2, 8, 128), F32),
            pltpu.VMEM((NL, 64, 128), BF16),
            pltpu.VMEM((128, 128), F32),
            pltpu.VMEM((NC, NL, 256, 128), BF16),
            pltpu.VMEM((NL, NR, 64, 128), BF16),
            pltpu.VMEM((640, 128), F32),
            pltpu.VMEM((128, 128), F32),
            pltpu.VMEM((NG, 256), BF16),
            pltpu.VMEM((NG, 128), F32),
            pltpu.VMEM((NG, 128), F32),
            pltpu.VMEM((NG, 256), F32),
            pltpu.VMEM((EX * EY, NG), BF16),
            pltpu.VMEM((EX * EY, NG), BF16),
            pltpu.VMEM((EX, EY, 128), F32),
            pltpu.VMEM((16, 640), F32),
            pltpu.VMEM((128, 384), F32),
            pltpu.VMEM((2, 4, EY, 128), F32),
            pltpu.VMEM((2, 16, 8, 128), F32),
            pltpu.VMEM((2, 128, 256), F32),
            pltpu.SemaphoreType.DMA((n_sem,)),
            pltpu.SemaphoreType.DMA((n_sem,)),
            pltpu.SemaphoreType.DMA((11,)),
        ],
        compiler_params=pltpu.CompilerParams(collective_id=0, has_side_effects=True),
    )(
        p_slabs[0], jnp.transpose(p_mask[0]), h_slabs[0], h_mask[0],
        gauss_row.reshape(8, 128), gauss_col.reshape(8, 128), gauss_cell.reshape(8, 128),
        gauss_expo.reshape(8, 128), gauss_pref.reshape(8, 128),
    )


def solution(mesh):
    placed = (
        P("layer", "row", "col"),
        P("layer", "row", "col"),
        P("layer", "row", "col"),
        P("layer", "row", "col"),
        P(("row", "col", "layer")),
        P(("row", "col", "layer")),
        P(("row", "col", "layer")),
        P(("row", "col", "layer")),
        P(("row", "col", "layer")),
    )
    return jax.shard_map(
        on_device,
        mesh=mesh,
        in_specs=placed,
        out_specs=(P("row", ("col", "layer")), P("row", "col", "layer")),
        check_vma=False,
    )
```

```python
import jax
import jax.numpy as jnp
from jax import lax
from jax.experimental import pallas as pl
from jax.experimental.pallas import tpu as pltpu
from jax.sharding import PartitionSpec as P

BS = 32
GX = 16
GY = 16
GZ = 128
R = 4
NG = 1024
NR = 16
NC = 8
NL = 4
EX = GX + 2 * R
EY = GY + 2 * R
F32 = jnp.float32
BF16 = jnp.bfloat16


def kernel(
    p_hbm, pm_hbm, h_hbm, hm_hbm, row_hbm, gcol_hbm, cell_hbm, expo_hbm, pref_hbm, prod_ref, dens_ref,
    p_in, pm_in, h_in, hm_in, g_int, g_float, h_ref, turn, pall, hall, gpad, gcols, onehot, colb, acc, ez, plane_hi, plane_lo, dens, rim, rim_in, row_in, col_in, side_in,
    send, recv, local,
):
    r = lax.axis_index("row")
    c = lax.axis_index("col")
    l = lax.axis_index("layer")
    row_of = lambda d: lax.rem(r + (d + NR), NR)
    col_of = lambda d: lax.rem(c + (d + NC), NC)
    lay_of = lambda d: lax.rem(l + (d + NL), NL)
    odd = lax.rem(c, 2)
    sib = c + 1 - 2 * odd
    out = c - 1 + 2 * odd
    other = lax.rem(out + NC, NC)

    loads = [
        pltpu.make_async_copy(src, dst, local.at[2 + n])
        for n, (src, dst) in enumerate(
            [(p_hbm, p_in), (pm_hbm, pm_in), (h_hbm, h_in), (hm_hbm, hm_in), (row_hbm, g_int.at[0]), (gcol_hbm, g_int.at[1]),
             (cell_hbm, g_int.at[2]), (expo_hbm, g_float.at[0]), (pref_hbm, g_float.at[1])]
        )
    ]
    for copy in loads:
        copy.start()
    barrier = pltpu.get_barrier_semaphore()
    peers = (
        [{"layer": lay_of(d)} for d in (1, 2, 3)]
        + [{"col": col_of(2 * d)} for d in (1, 2, 3)]
        + [{"col": sib}, {"col": other}]
        + [{"row": row_of(d)} for d in (1, -1, 2, -2)]
        + [{"row": row_of(a), "layer": lay_of(b)} for a in (1, -1) for b in (1, -1)]
    )
    for peer in peers:
        pl.semaphore_signal(barrier, inc=1, device_id=peer, device_id_type=pl.DeviceIdType.MESH)
    block = lax.broadcasted_iota(jnp.int32, (4, 128), 0)
    of_lane = lax.broadcasted_iota(jnp.int32, (4, 128), 1) // BS
    loads[0].wait()
    loads[1].wait()
    for i in range(256 // BS):
        column = jnp.broadcast_to(pm_in[:, i : i + 1], (4, 128))
        keep = jnp.sum(jnp.where(block == of_lane, column, 0), axis=0, keepdims=True) > 0
        rows = slice(i * BS, (i + 1) * BS)
        value = jnp.where(jnp.broadcast_to(keep, (BS, 128)), p_in[rows, :].astype(F32), 0.0)
        pall[c, l, rows, :] = value.astype(BF16)
    loads[2].wait()
    loads[3].wait()
    of_lane = lax.broadcasted_iota(jnp.int32, (1, 128), 1) // BS
    for q in range(NL):
        for i in range(64 // BS):
            keep = jnp.zeros((1, 128), jnp.int32)
            for j in range(4):
                at = q * 4 + j
                keep = jnp.where(of_lane == j, jnp.broadcast_to(hm_in[i : i + 1, at : at + 1], (1, 128)), keep)
            rows = slice(i * BS, (i + 1) * BS)
            value = h_in[rows, q * 128 : (q + 1) * 128].astype(F32)
            value = jnp.where(jnp.broadcast_to(keep > 0, (BS, 128)), value, 0.0)
            h_ref[q, rows, :] = value.astype(BF16)
    own_h = pltpu.make_async_copy(h_ref.at[l], hall.at[l, r], local.at[1])
    own_h.start()
    p_ref = pall.at[c, l]
    pl.semaphore_wait(barrier, len(peers))

    pending = []
    slots = {}

    def push(key, src, dst, peer):
        n = slots.setdefault(key, len(slots))
        copy = pltpu.make_async_remote_copy(
            src_ref=src, dst_ref=dst, send_sem=send.at[n], recv_sem=recv.at[n],
            device_id=peer, device_id_type=pl.DeviceIdType.MESH,
        )
        copy.start()
        pending.append(copy)
        return copy

    low = pl.ds(0, 128)
    high = pl.ds(128, 128)
    copies = {}
    right = {"row": row_of(1)}
    left = {"row": row_of(-1)}
    order = (0, 1, 3, 2)
    tree = [
        (0, 2), (0, -2), (0, 1), (0, -1), (2, 4), (-2, -4), (2, 3), (-2, -3),
        (4, 6), (-4, -6), (4, 5), (-4, -5), (6, 8), (6, 7), (-6, -7),
    ]

    def spread(parent, d):
        if parent:
            copies["h", parent, d].wait_recv()
        for source, target in tree:
            if source == parent:
                piece = hall.at[lay_of(-d), row_of(-parent)]
                peer = {"row": row_of(target - parent)}
                copies["h", target, d] = push(("h", target, d), piece, piece, peer)

    def hop(parent):
        for d in order:
            spread(parent, d)
            spread(-parent, d)

    for d in (1, 3, 2):
        copies["ha", d] = push(("ha", d), h_ref.at[lay_of(d)], hall.at[l, r], {"layer": lay_of(d)})
    own_h.wait()
    spread(0, 0)
    for d in (1, 3, 2):
        copies["py", d] = push(("py", d), p_ref, pall.at[c, l], {"layer": lay_of(d)})
        copies["px", d] = push(("px", d), p_ref, pall.at[c, l], {"col": col_of(2 * d)})
    copies["ps"] = push(("ps",), p_ref, pall.at[c, l], {"col": sib})

    for copy in loads[4:]:
        copy.wait()
    cell = g_int[2]
    turn[0:8, :] = g_int[0].astype(F32)
    turn[8:16, :] = g_int[1].astype(F32)
    turn[16:24, :] = (cell & (GZ - 1)).astype(F32)
    turn[24:32, :] = g_float[0]
    turn[32:40, :] = g_float[1]
    turn[40:128, :] = jnp.zeros((88, 128), F32)
    gcols[...] = jnp.transpose(turn[...])

    for d in order[1:]:
        copies["ha", d].wait_recv()
        spread(0, d)
    lane = lax.broadcasted_iota(jnp.int32, (128, 256), 1)
    lane_f = lane.astype(F32)
    pos_z = jnp.where(lane < 136, lane, lane - 144).astype(F32)
    near_z = (lane < 132) | ((lane >= 140) & (lane < 144))
    for k in range(NG // 128):
        rows = slice(k * 128, (k + 1) * 128)
        onehot[rows, :] = jnp.where(gcols[:, k : k + 1] == lane_f, 1.0, 0.0).astype(BF16)
        colb[rows, :] = gcols[:, 8 + k : 9 + k] - lane_f[:, :128]
        acc[rows, :] = jnp.zeros((128, 128), F32)

    def lookup(tiles):
        refs = [(pall.at[a, b], (b * NG + a * 128).astype(F32)) for a, b in tiles]

        def body(k, _):
            rows = pl.ds(pl.multiple_of(k * 256, 256), 256)
            hot = onehot[rows, :]
            want = colb[rows, :]
            total = acc[rows, :]
            for ref, base in refs:
                found = jnp.dot(hot, ref[...], preferred_element_type=F32)
                total = total + jnp.where(want == base, found, 0.0)
            acc[rows, :] = total
            return 0

        lax.fori_loop(0, NG // 256, body, 0)

    for d in (1, 3, 2):
        copies["py", d].wait_recv()
        tile = pall.at[c, lay_of(-d)]
        for e in (1, 3, 2):
            part = tile.at[low]
            copies["a", d, e] = push(("a", d, e), part, part, {"col": col_of(2 * e)})
        copies["sy", d] = push(("sy", d), tile, tile, {"col": sib})
        copies["px", d].wait_recv()
        tile = pall.at[col_of(-2 * d), l]
        for e in (1, 3, 2):
            part = tile.at[high]
            copies["b", d, e] = push(("b", d, e), part, part, {"layer": lay_of(e)})
        copies["sx", d] = push(("sx", d), tile, tile, {"col": sib})

    pos = lax.broadcasted_iota(jnp.int32, (EX, 128), 0)
    pos = jnp.where(pos < 20, pos, pos - 24).astype(F32)
    for k in range(NG // 128):
        rows = slice(k * 128, (k + 1) * 128)
        dz = pos_z - gcols[:, 16 + k : 17 + k]
        value = jnp.exp(-gcols[:, 24 + k : 25 + k] * dz * dz)
        ez[rows, :] = jnp.where(near_z & (jnp.abs(dz) <= R), value, 0.0)

    def make_plane(k, _):
        cols = pl.ds(pl.multiple_of(k * 128, 128), 128)
        at = g_int[2, pl.ds(k, 1), :]
        expo = g_float[0, pl.ds(k, 1), :]
        dx = pos - (at >> 11).astype(F32)
        ex = jnp.where(jnp.abs(dx) <= R, jnp.exp(-expo * dx * dx), 0.0)
        dy = pos - ((at >> 7) & (GY - 1)).astype(F32)
        ey = jnp.where(jnp.abs(dy) <= R, jnp.exp(-expo * dy * dy), 0.0)
        for i in range(0, EX, 2):
            value = jnp.concatenate([ex[i : i + 1, :] * ey, ex[i + 1 : i + 2, :] * ey], axis=0)
            upper = value.astype(BF16)
            plane_hi[i * EY : (i + 2) * EY, cols] = upper
            plane_lo[i * EY : (i + 2) * EY, cols] = (value - upper.astype(F32)).astype(BF16)
        return 0

    lax.fori_loop(0, NG // 128, make_plane, 0)
    lookup([(c, l)] + [(c, lay_of(-d)) for d in (1, 3, 2)] + [(col_of(-2 * d), l) for d in (1, 3, 2)])
    hop(2)

    copies["ps"].wait_recv()
    for d in (1, 3, 2):
        copies["sy", d].wait_recv()
        copies["sx", d].wait_recv()
    sib_of = lambda d: lax.rem(sib + (d + NC), NC)
    lookup([(sib, l)] + [(sib, lay_of(-d)) for d in (1, 3, 2)] + [(sib_of(-2 * d), l) for d in (1, 3, 2)])

    for d in (1, 3, 2):
        for e in (1, 3, 2):
            copies["a", d, e].wait_recv()
            part = pall.at[col_of(-2 * e), lay_of(-d), low]
            copies["sa", d, e] = push(("sa", d, e), part, part, {"col": sib})
            copies["b", d, e].wait_recv()
            part = pall.at[col_of(-2 * d), lay_of(-e), high]
            copies["sb", d, e] = push(("sb", d, e), part, part, {"col": sib})
    corners = [(d, e) for d in (1, 3, 2) for e in (1, 3, 2)]
    lookup([(col_of(-2 * d), lay_of(-e)) for d, e in corners])
    hop(4)
    for d, e in corners:
        copies["sa", e, d].wait_recv()
        copies["sb", d, e].wait_recv()
        if e == 2:
            lookup([(sib_of(-2 * d), lay_of(-f)) for f in (1, 3, 2)])

    for k in range(NG // 128):
        rows = slice(k * 128, (k + 1) * 128)
        coef = jnp.sum(acc[rows, :], axis=1, keepdims=True) * gcols[:, 32 + k : 33 + k]
        ez[rows, :] = ez[rows, :] * coef

    depth = ez[...]
    depth_hi = depth.astype(BF16)
    depth_lo = (depth - depth_hi.astype(F32)).astype(BF16)
    step = 4 * EY
    for k in range(EX // 4):
        rows = slice(k * step, (k + 1) * step)
        part = jnp.dot(plane_hi[rows, :], depth_lo, preferred_element_type=F32)
        part = part + jnp.dot(plane_lo[rows, :], depth_hi, preferred_element_type=F32)
        part = part + jnp.dot(plane_hi[rows, :], depth_hi, preferred_element_type=F32)
        dens[k * 4 : (k + 1) * 4] = part[:, :128].reshape(4, EY, 128)
        gpad[rows, :] = part[:, 128:]
    gpad[EX * EY : 640, :] = jnp.zeros((64, 128), F32)
    for k in range(5):
        turned = jnp.transpose(gpad[k * 128 : (k + 1) * 128, :])
        rim[:, k * 128 : (k + 1) * 128] = turned[0:16, :]
    for n in range(2):
        side_in[n, 8:120, :] = jnp.zeros((112, 256), F32)
    rim_in[8:120, :] = jnp.zeros((112, 384), F32)
    up = {"layer": lay_of(1)}
    down = {"layer": lay_of(-1)}
    copies["ru"] = push(("ru",), dens.at[16:20], row_in.at[0], right)
    copies["rd"] = push(("rd",), dens.at[20:24], row_in.at[1], left)
    copies["lu"] = push(("lu",), rim.at[0:8, 0:384], rim_in.at[0:8], up)
    copies["ld"] = push(("ld",), rim.at[8:16, 0:384], rim_in.at[120:128], down)
    for n, step in enumerate((1, -1)):
        for name, dz, rows, into in (("u", 1, slice(0, 8), slice(0, 8)), ("d", -1, slice(8, 16), slice(120, 128))):
            peer = {"row": row_of(step), "layer": lay_of(dz)}
            copies["s", n, name] = push(("s", n, name), rim.at[rows, 384:640], side_in.at[n, into], peer)
    hop(6)

    for k in ("ru", "rd", "lu", "ld"):
        copies[k].wait_recv()
    for k in range(3):
        gpad[k * 128 : (k + 1) * 128, :] = jnp.transpose(rim_in[:, k * 128 : (k + 1) * 128])
    for k in range(GX):
        dens[k] = dens[k] + gpad[k * EY : (k + 1) * EY, :]
    for n, at in ((0, 0), (1, 12)):
        copies["s", n, "u"].wait_recv()
        copies["s", n, "d"].wait_recv()
        for k in range(2):
            gpad[384 + k * 128 : 512 + k * 128, :] = jnp.transpose(side_in[n, :, k * 128 : (k + 1) * 128])
        for k in range(4):
            here = 384 + (n * 4 + k) * EY
            dens[at + k] = dens[at + k] + gpad[here : here + EY, :]
    dens[0:4] = dens[0:4] + row_in[0]
    dens[12:16] = dens[12:16] + row_in[1]
    edge = dens.at[0:16, 16:24]
    copies["cu"] = push(("cu",), edge, col_in.at[0], {"col": col_of(1)})
    copies["cd"] = push(("cd",), edge, col_in.at[1], {"col": col_of(-1)})
    for leaf in (1, -1, 3, -3, 5, -5, 7, -7, 8):
        for d in order:
            copies["h", leaf, d].wait_recv()

    total = jnp.zeros((256, 128), F32)
    for b in range(NL):
        for k in range(NC // 2):
            lhs = jnp.concatenate([pall[2 * k, b], pall[2 * k + 1, b]], axis=1)
            rhs = hall[b, 4 * k : 4 * k + 4].reshape(256, 128)
            total = total + jnp.dot(lhs, rhs, preferred_element_type=F32)
    prod_ref[...] = total.astype(BF16)

    copies["cu"].wait_recv()
    copies["cd"].wait_recv()
    inner = lax.broadcasted_iota(jnp.int32, (16, 8, 128), 1)
    dens_ref[:, 0:8, :] = dens[0:16, 0:8, :] + jnp.where(inner < 4, col_in[0], 0.0)
    dens_ref[:, 8:16, :] = dens[0:16, 8:16, :] + jnp.where(inner >= 4, col_in[1], 0.0)
    for copy in pending:
        copy.wait_send()


def on_device(
    p_slabs, p_mask, h_slabs, h_mask, gauss_row, gauss_col, gauss_cell, gauss_expo, gauss_pref
):
    n_sem = 128
    vmem = pl.BlockSpec(memory_space=pltpu.VMEM)
    return pl.pallas_call(
        kernel,
        out_shape=(
            jax.ShapeDtypeStruct((256, 128), BF16),
            jax.ShapeDtypeStruct((GX, GY, GZ), F32),
        ),
        in_specs=[pl.BlockSpec(memory_space=pl.ANY)] * 9,
        out_specs=(vmem, vmem),
        scratch_shapes=[
            pltpu.VMEM((256, 128), BF16),
            pltpu.VMEM((4, 8), jnp.int32),
            pltpu.VMEM((64, 512), BF16),
            pltpu.VMEM((2, 16), jnp.int32),
            pltpu.VMEM((3, 8, 128), jnp.int32),
            pltpu.VMEM((2, 8, 128), F32),
            pltpu.VMEM((NL, 64, 128), BF16),
            pltpu.VMEM((128, 128), F32),
            pltpu.VMEM((NC, NL, 256, 128), BF16),
            pltpu.VMEM((NL, NR, 64, 128), BF16),
            pltpu.VMEM((640, 128), F32),
            pltpu.VMEM((128, 128), F32),
            pltpu.VMEM((NG, 256), BF16),
            pltpu.VMEM((NG, 128), F32),
            pltpu.VMEM((NG, 128), F32),
            pltpu.VMEM((NG, 256), F32),
            pltpu.VMEM((EX * EY, NG), BF16),
            pltpu.VMEM((EX * EY, NG), BF16),
            pltpu.VMEM((EX, EY, 128), F32),
            pltpu.VMEM((16, 640), F32),
            pltpu.VMEM((128, 384), F32),
            pltpu.VMEM((2, 4, EY, 128), F32),
            pltpu.VMEM((2, 16, 8, 128), F32),
            pltpu.VMEM((2, 128, 256), F32),
            pltpu.SemaphoreType.DMA((n_sem,)),
            pltpu.SemaphoreType.DMA((n_sem,)),
            pltpu.SemaphoreType.DMA((11,)),
        ],
        compiler_params=pltpu.CompilerParams(collective_id=0, has_side_effects=True),
    )(
        p_slabs[0], jnp.transpose(p_mask[0]), h_slabs[0], h_mask[0],
        gauss_row.reshape(8, 128), gauss_col.reshape(8, 128), gauss_cell.reshape(8, 128),
        gauss_expo.reshape(8, 128), gauss_pref.reshape(8, 128),
    )


def solution(mesh):
    placed = (
        P("layer", "row", "col"),
        P("layer", "row", "col"),
        P("layer", "row", "col"),
        P("layer", "row", "col"),
        P(("row", "col", "layer")),
        P(("row", "col", "layer")),
        P(("row", "col", "layer")),
        P(("row", "col", "layer")),
        P(("row", "col", "layer")),
    )
    return jax.shard_map(
        on_device,
        mesh=mesh,
        in_specs=placed,
        out_specs=(P("row", ("col", "layer")), P("row", "col", "layer")),
        check_vma=False,
    )
```
